32 devices in a mesh: proj: 8 (over z, x), lang: 4 (over y, core).
Axes of the slice: x: 2, y: 2, z: 4, core: 2. Of those that a mesh axis runs over, the one named last changes fastest.
Arguments:
- mapped_layer_arguments: bfloat16 [48, 512, 8192], P('lang', None, 'proj'), may hold values from -6 to 6
- loss_slope_at_result: bfloat16 [48, 512, 8192], P('lang', None, 'proj'), may hold values from -6 to 6
- left_lowrank_weights: bfloat16 [8192, 128], P('proj'), may hold values from -0.0625 to 0.0625
- right_lowrank_weights: bfloat16 [128, 8192], P(None, 'proj'), may hold values from -0.0625 to 0.0625
- mean_estimate_left: float32 [8192, 128], P('proj'), may hold values from -24 to 24
- variance_estimate_left: float32 [8192, 128], P('proj'), may hold values from 0.1 to 10
- mean_estimate_right: float32 [128, 8192], P(None, 'proj'), may hold values from -24 to 24
- variance_estimate_right: float32 [128, 8192], P(None, 'proj'), may hold values from 0.1 to 10
- heldout_sketched_slopes: bfloat16 [8, 256, 8192], P('lang', None, 'proj'), may hold values from -600 to 600
- tongue_label_per_example: int32 [48, 1], P('lang'), may hold values from 0 to 7; in each aligned block of 12 rows (0 to 11, 12 to 23, ...) at most 3 rows name the same one
- heldout_example_tally: int32 [8], replicated, may hold values from 1 to 256, 1280 in all
- sketch_random_key: int32 [1], replicated, may hold values from 0 to 16777215
Outputs:
- features: float32 [48, 8192], P('lang', 'proj')
- scores: float32 [48], P('lang')
The draws below stay inside these ranges and needn't reach their ends.
Inputs may be any that keep to these rules, and one draw needn't show every extreme that they name: `tongue_label_per_example`: among the 12 samples of one device, in aligned blocks of rows, no language appears more than 3 times.
All inputs are finite; a program needn't handle non-finite values.
Results may differ from the reference program's by a relative error of at most 0.0049.
Values may be sent and summed in bfloat16 or wider, within the bound.
A program may use at most 128 MiB of HBM per device.

```python
import math
import jax
import jax.numpy as jnp
import numpy as np
from jax import lax

HIDDEN_FEATURES = 8192
LOWRANK_INNER = 128
K = 8192
TOK = 512
SAMP_DEV = 12
NVAL = 256
MOST = 3
LANGS = 8
SAMPLES = 48


def draw_heldout_sketched_slopes(key, part):
    key_base, key_rows, key_cols = jax.random.split(key, 3)
    full_shape = (LANGS, NVAL, K)
    base_values = jnp.clip(jax.random.normal(key_base, full_shape, jnp.float32), -6.0, 6.0)
    row_scale = jnp.exp(jax.random.uniform(key_rows, (LANGS, NVAL, 1), jnp.float32, 0.0, math.log(10.0)))
    col_scale = jnp.exp(jax.random.uniform(key_cols, (1, 1, K), jnp.float32, 0.0, math.log(10.0)))
    return (base_values * row_scale * col_scale).astype(jnp.bfloat16)


def block_scale(rng, extent, shards, least, top_value):
    def one(position, blocks):
        heights = jax.random.uniform(jax.random.fold_in(jax.random.fold_in(rng, 6), position), (blocks,), jnp.float32, least / len(shards), top_value / len(shards))
        return jnp.repeat(jnp.exp(heights), extent[position] // blocks).reshape((-1,) + (1,) * (len(extent) - position - 1))

    factor_of = one(*shards[0])
    for cut in shards[1:]:
        factor_of = factor_of * one(*cut)
    return factor_of


def profile(amount, total, limit, lean):
    weights = [(1 << 20) // math.isqrt(grade ** lean) + 1 for grade in range(2, amount + 1)]
    spare, holding = total - limit - (amount - 1), [1] * (amount - 1)
    while spare > 0:
        candidates = [i for i in range(amount - 1) if holding[i] < limit]
        pool, remaining = sum([weights[i] for i in candidates]), spare
        for i in candidates:
            extra = min(limit - holding[i], max(1, remaining * weights[i] // pool), spare)
            holding[i] = holding[i] + extra
            spare = spare - extra
    return np.array([limit] + holding)


def uneven_parts(key, count, total, limit, lean):
    if count == 2:
        one = jax.random.randint(key, (), max(1, total - limit), min(limit, total - 1) + 1)
        return jnp.stack([one, total - one])
    lengths = jnp.asarray(profile(count, total, limit, lean), jnp.int32)
    couples = (count - 1) // 2
    giver, sink = lengths[1:1 + 2 * couples:2], lengths[2:2 + 2 * couples:2]
    slack = jnp.minimum(giver - 1, limit - sink)
    shifted = jax.random.randint(jax.random.fold_in(key, 1), (couples,), 0, 1 << 20) % (slack + 1)
    lengths = lengths.at[1:1 + 2 * couples:2].set(giver - shifted).at[2:2 + 2 * couples:2].set(sink + shifted)
    return lengths[jax.random.permutation(jax.random.fold_in(key, 2), count)]


def assign_block(stream_key, own, number, rows, number_of, top, reach, skew):
    sequence = jax.random.permutation(stream_key, number_of)
    crowded, ordinary = load_shares(number_of, rows * top, reach, skew, True), load_shares(number_of, rows * top, reach, skew, False)
    places = jnp.arange(number_of)

    def named(sizes, offset_by):
        used = int((sizes > 0).sum())
        fixed = max(1, used // 4)
        passed = fixed + (places - fixed + offset_by * (used - fixed)) % max(1, number_of - fixed)
        return jnp.zeros((number_of,), jnp.int32).at[sequence[jnp.where(places < fixed, places, passed)]].set(jnp.asarray(sizes, jnp.int32))

    sizes = jnp.where(number % 4 == 0, named(crowded, number // 4), named(ordinary, number - number // 4 - 1))
    mixed = jax.random.permutation(jax.random.fold_in(own, 3), number_of)
    source_of, sink = mixed[0:number_of // 2 * 2:2], mixed[1:number_of // 2 * 2:2]
    room = jnp.minimum(sizes[source_of] - 1, reach - sizes[sink]) // 2
    room = jnp.where((source_of == sequence[0]) | (sink == sequence[0]) | (sizes[sink] == 0), 0, jnp.maximum(room, 0))
    passed = jax.random.randint(jax.random.fold_in(own, 4), (number_of // 2,), 0, 1 << 20) % (room + 1)
    sizes = sizes.at[source_of].add(-passed).at[sink].add(passed)
    items = jnp.searchsorted(jnp.cumsum(sizes), jnp.arange(rows * top), side="right").astype(jnp.int32)
    grid = items.reshape(top, rows).T
    grid = grid[jax.random.permutation(jax.random.fold_in(own, 1), rows)]
    offset_by = jax.random.randint(jax.random.fold_in(own, 2), (rows, 1), 0, top)
    return jnp.take_along_axis(grid, (jnp.arange(top)[None, :] + offset_by) % top, axis=1)


def load_shares(number_of, total, reach, skew, full):
    weights = [(1 << 20) // math.isqrt(rank ** skew) + 1 for rank in range(1, number_of + 1)]
    largest = reach if full else min(reach, max(-(-total // number_of), total * weights[0] // sum(weights)))
    least = 1 if total - largest >= number_of - 1 else 0
    counts, surplus = [largest] + [least] * (number_of - 1), total - largest - least * (number_of - 1)
    while surplus > 0:
        movable = [i for i in range(1, number_of) if counts[i] < largest] or [i for i in range(1, number_of) if counts[i] < reach]
        mass, budget = sum([weights[i] for i in movable]), surplus
        for i in movable:
            more = min(reach - counts[i], max(1, budget * weights[i] // mass), surplus)
            counts[i] = counts[i] + more
            surplus = surplus - more
    return np.array(counts)


def gaussian(own_key, shape, scale, most, pieces=(), held_as=jnp.bfloat16):
    values = scale * jax.random.normal(own_key, shape, jnp.float32)
    if pieces:
        values = values * block_scale(own_key, shape, pieces, -0.22, 0.18)
    return jnp.clip(values, -most, most).astype(held_as)


def setup_inputs(seed: int = 0) -> dict:
    key_list = jax.random.split(jax.random.key(seed), 13)
    mapped_layer_arguments = gaussian(key_list[0], (SAMPLES, TOK, HIDDEN_FEATURES), 1.0, 6.0, ((0, 4), (2, 8)))
    loss_slope_at_result = gaussian(key_list[1], (SAMPLES, TOK, HIDDEN_FEATURES), 1.0, 6.0, ((0, 4), (2, 8)))
    left_lowrank_weights = gaussian(key_list[2], (HIDDEN_FEATURES, LOWRANK_INNER), HIDDEN_FEATURES ** -0.5, 0.0625, ((0, 8),))
    right_lowrank_weights = gaussian(key_list[3], (LOWRANK_INNER, HIDDEN_FEATURES), HIDDEN_FEATURES ** -0.5, 0.0625, ((1, 8),))
    mean_estimate_left = gaussian(key_list[4], (HIDDEN_FEATURES, LOWRANK_INNER), 4.0, 24.0, ((0, 8),), jnp.float32)
    variance_estimate_left = jnp.clip(jnp.exp(math.log(10.0) - 4.6051702 * jax.random.uniform(key_list[5], (HIDDEN_FEATURES, LOWRANK_INNER), jnp.float32) ** block_scale(key_list[5], (HIDDEN_FEATURES, LOWRANK_INNER), ((0, 8),), -0.2, 0.2)), 0.1, 10.0)
    mean_estimate_right = gaussian(key_list[6], (LOWRANK_INNER, HIDDEN_FEATURES), 4.0, 24.0, ((1, 8),), jnp.float32)
    variance_estimate_right = jnp.clip(jnp.exp(math.log(10.0) - 4.6051702 * jax.random.uniform(key_list[7], (LOWRANK_INNER, HIDDEN_FEATURES), jnp.float32) ** block_scale(key_list[7], (LOWRANK_INNER, HIDDEN_FEATURES), ((1, 8),), -0.2, 0.2)), 0.1, 10.0)
    heldout_sketched_slopes = draw_heldout_sketched_slopes(jax.random.fold_in(key_list[12], 71), 0)
    tongue_label_per_example_keys = jax.random.split(jax.random.fold_in(key_list[9], 1), SAMPLES // SAMP_DEV)
    tongue_label_per_example_turns = jax.random.permutation(jax.random.fold_in(key_list[9], 3), SAMPLES // SAMP_DEV)
    tongue_label_per_example = jax.vmap(lambda own, number: assign_block(jax.random.fold_in(key_list[9], 2), own, number, SAMP_DEV, LANGS, 1, MOST, 2))(tongue_label_per_example_keys, tongue_label_per_example_turns).reshape((SAMPLES, 1))
    heldout_example_tally = uneven_parts(key_list[10], LANGS, 5 * NVAL, NVAL, 2).astype(jnp.int32)
    sketch_random_key = jax.random.randint(key_list[11], (1,), 0, 16777216).astype(jnp.int32)
    return {"mapped_layer_arguments": mapped_layer_arguments, "loss_slope_at_result": loss_slope_at_result, "left_lowrank_weights": left_lowrank_weights, "right_lowrank_weights": right_lowrank_weights, "mean_estimate_left": mean_estimate_left, "variance_estimate_left": variance_estimate_left, "mean_estimate_right": mean_estimate_right, "variance_estimate_right": variance_estimate_right, "heldout_sketched_slopes": heldout_sketched_slopes, "tongue_label_per_example": tongue_label_per_example, "heldout_example_tally": heldout_example_tally, "sketch_random_key": sketch_random_key}


update_multiplier = 1.25

def scramble(hashed):
    hashed = jnp.bitwise_xor(hashed, lax.shift_right_logical(hashed, jnp.int32(16)))
    hashed = hashed * 2146121005
    hashed = jnp.bitwise_xor(hashed, lax.shift_right_logical(hashed, jnp.int32(15)))
    hashed = hashed * 739982445
    hashed = jnp.bitwise_xor(hashed, lax.shift_right_logical(hashed, jnp.int32(16)))
    return hashed

def sign_table(seed_value, table_id, row_count, row_start, col_count):
    row_ids = (row_start + lax.iota(jnp.int32, row_count)).astype(jnp.int32)
    col_ids = lax.iota(jnp.int32, col_count)
    anchor = scramble((seed_value * 4 + table_id).astype(jnp.int32))
    hashed = scramble(anchor + row_ids[:, None] * col_count + col_ids[None, :])
    sign_bit = jnp.bitwise_and(lax.shift_right_logical(hashed, jnp.int32(13)), 1)
    return (1 - 2 * sign_bit).astype(jnp.float32)

def precondition(gradient, moment, second):
    return ((0.9 * moment + 0.1 * gradient) * lax.rsqrt(0.999 * second + 0.001 * gradient * gradient)).astype(jnp.bfloat16)

def reference(mapped_layer_arguments, loss_slope_at_result, left_lowrank_weights, right_lowrank_weights, mean_estimate_left, variance_estimate_left, mean_estimate_right, variance_estimate_right, heldout_sketched_slopes, tongue_label_per_example, heldout_example_tally, sketch_random_key):
    seed_value = sketch_random_key[0].astype(jnp.int32)
    anchor_row = jnp.int32(0)
    up_left = sign_table(seed_value, 0, LOWRANK_INNER, anchor_row, K)
    up_right = sign_table(seed_value, 1, HIDDEN_FEATURES, anchor_row, K)
    down_left = sign_table(seed_value, 2, HIDDEN_FEATURES, anchor_row, K)
    down_right = sign_table(seed_value, 3, LOWRANK_INNER, anchor_row, K)

    def one_sample(sample_pair):
        entering_signals, output_slope_gathered = sample_pair
        entering_signal_accumulated = (update_multiplier * jnp.dot(entering_signals, left_lowrank_weights, preferred_element_type=jnp.float32)).astype(jnp.bfloat16)
        output_slope_accumulated = (update_multiplier * jnp.dot(output_slope_gathered, right_lowrank_weights.T, preferred_element_type=jnp.float32)).astype(jnp.bfloat16)
        grad_up = jnp.dot(entering_signal_accumulated.T, output_slope_gathered, preferred_element_type=jnp.float32)
        grad_down = jnp.dot(entering_signals.T, output_slope_accumulated, preferred_element_type=jnp.float32)
        step_up = precondition(grad_up, mean_estimate_right, variance_estimate_right)
        step_down = precondition(grad_down, mean_estimate_left, variance_estimate_left)
        mixed_up = jnp.dot(step_up.astype(jnp.float32), up_right, precision=lax.Precision.HIGHEST)
        mixed_down = jnp.dot(step_down.T.astype(jnp.float32), down_left, precision=lax.Precision.HIGHEST)
        return lax.optimization_barrier(jnp.sum(mixed_up * up_left + mixed_down * down_right, axis=0))
    projected = lax.map(one_sample, (mapped_layer_arguments, loss_slope_at_result))
    features = projected * lax.rsqrt(lax.optimization_barrier(jnp.mean(projected * projected, axis=-1, keepdims=True)) + 1e-06)
    feat_low = features.astype(jnp.bfloat16)
    val_wide = heldout_sketched_slopes.astype(jnp.float32)
    val_rms = jnp.sqrt(lax.optimization_barrier(jnp.mean(val_wide * val_wide, axis=-1)) + 1e-06)
    lang_of = tongue_label_per_example[:, 0].astype(jnp.int32)
    flat_val = heldout_sketched_slopes.reshape(LANGS * NVAL, K)
    dot_sums = jnp.dot(feat_low, flat_val.T, preferred_element_type=jnp.float32).reshape(SAMPLES, LANGS, NVAL)
    similar = dot_sums / (math.sqrt(K) * val_rms[None, :, :])
    own_sim = jnp.take_along_axis(similar, lang_of[:, None, None], axis=1)[:, 0, :]
    own_count = heldout_example_tally[lang_of]
    is_valid = lax.iota(jnp.int32, NVAL)[None, :] < own_count[:, None]
    scores = lax.optimization_barrier(jnp.max(jnp.where(is_valid, own_sim, jnp.float32(-1e+30)), axis=-1))
    return (features, scores)
```

```python
import functools
import math

import jax
import jax.numpy as jnp
from jax import lax
from jax.experimental import pallas as pl
from jax.experimental.pallas import tpu as pltpu
from jax.sharding import PartitionSpec as P

RANK = 128
UPDATE_MULTIPLIER = 1.25
M1 = 2146121005
M2_UP = (739982445 * 4 + 2**31) % 2**32 - 2**31
MESH = pl.DeviceIdType.MESH

PAIR = 2
SLOTS = 3
GROUP = PAIR * SLOTS
STEP, WIDE = 16, 512
TILE = 512


def scramble(hashed):
    hashed = jnp.bitwise_xor(hashed, lax.shift_right_logical(hashed, jnp.int32(16)))
    hashed = hashed * 2146121005
    hashed = jnp.bitwise_xor(hashed, lax.shift_right_logical(hashed, jnp.int32(15)))
    hashed = hashed * 739982445
    hashed = jnp.bitwise_xor(hashed, lax.shift_right_logical(hashed, jnp.int32(16)))
    return hashed


def signs(h):
    h = h ^ lax.shift_right_logical(h, jnp.int32(16))
    h = h * jnp.int32(M1)
    h = h ^ lax.shift_right_logical(h, jnp.int32(15))
    h = h * jnp.int32(M2_UP)
    h = h ^ lax.shift_left(h, jnp.int32(16))
    return jnp.where(h < 0, jnp.float32(-1.0), jnp.float32(1.0)).astype(jnp.bfloat16)


def main_kernel(
    shards, cols,
    base_ref, left_ref, right_ref, mean_l_ref, var_l_ref, mean_r_ref, var_r_ref, in_ref, gr_ref,
    raw_ref,
    table, wide, weights, mean_t, var_t, keep, away, pair, mine, land, low, step, acc, pieces,
    load, xs, xr, zs, zr, gs, gr, ys, yr, ps, pr,
):
    me = lax.axis_index("proj")
    rest = shards // 2
    x, z = lax.rem(me, 2), me // 2
    n, tok, w = in_ref.shape
    chunks = n // PAIR
    total = 2 * chunks
    groups = n // GROUP
    piece = tok // rest
    partner = z * 2 + (1 - x)
    others = [lax.rem(z + d, rest) for d in range(1, rest)]
    down_row = w + 2 * RANK

    def span(start, size):
        return pl.ds(pl.multiple_of(start, 16), size)

    def loaded(source, c, slot):
        return pltpu.make_async_copy(
            source.at[pl.ds(c * PAIR, PAIR)], wide.at[slot], load.at[slot]
        )

    for c in range(SLOTS):
        loaded(in_ref, c, c).start()

    barrier = pltpu.get_barrier_semaphore()
    for d in range(1, shards):
        pl.semaphore_signal(
            barrier, inc=1, device_id={"proj": lax.rem(me + d, shards)}, device_id_type=MESH
        )

    weights[0] = left_ref[...]
    weights[1] = right_ref[...].astype(jnp.float32).T.astype(jnp.bfloat16)
    mean_t[...] = mean_l_ref[...].T
    var_t[...] = var_l_ref[...].T
    pl.semaphore_wait(barrier, shards - 1)

    def remote(src, dst, send, recv, target):
        return pltpu.make_async_remote_copy(
            src_ref=src, dst_ref=dst, send_sem=send, recv_sem=recv,
            device_id={"proj": target}, device_id_type=MESH,
        )

    def first(c):
        return remote(away.at[c], pair.at[c], xs.at[c], xr.at[c], partner)

    def second(c, d):
        s = c * (rest - 1) + d - 1
        return remote(
            mine.at[c, span(others[d - 1] * piece, piece)], land.at[s],
            zs.at[s], zr.at[s], others[d - 1] * 2 + x,
        )

    def third(c, d):
        s = c * (rest - 1) + d - 1
        where = span((c % chunks) * PAIR * tok + x * tok + z * piece, piece)
        return remote(
            low.at[c // chunks, where], low.at[c // chunks, where],
            gs.at[s], gr.at[s], others[d - 1] * 2 + x,
        )

    def fourth(c):
        where = span((c % chunks) * PAIR * tok + x * tok, tok)
        return remote(
            low.at[c // chunks, where], low.at[c // chunks, where], ys.at[c], yr.at[c], partner
        )

    def job0(c):
        first(c).start()

    def job1(c):
        first(c).wait_recv()
        mine[c] = (keep[c] + pair[c].astype(jnp.float32)).astype(jnp.bfloat16)
        for d in range(1, rest):
            second(c, d).start()

    def job2(c):
        for d in range(1, rest):
            second(c, d).wait_recv()
        summed = mine[c, span(z * piece, piece), :].astype(jnp.float32)
        for d in range(1, rest):
            summed = summed + land[c * (rest - 1) + d - 1].astype(jnp.float32)
        where = span((c % chunks) * PAIR * tok + x * tok + z * piece, piece)
        low[c // chunks, where, :] = (UPDATE_MULTIPLIER * summed).astype(jnp.bfloat16)
        for d in range(1, rest):
            third(c, d).start()

    def job3(c):
        for d in range(1, rest):
            third(c, d).wait_recv()
        fourth(c).start()

    def job4(c):
        fourth(c).wait_recv()

    def run(jobs, tick):
        for when, job, c in jobs:
            @pl.when(tick == when)
            def _():
                job(c)

    local = lax.broadcasted_iota(jnp.int32, (STEP, WIDE), 0) * cols + lax.broadcasted_iota(
        jnp.int32, (STEP, WIDE), 1
    )
    run_cols = 4 * WIDE
    per_row = cols // run_cols
    units = (down_row // STEP) * per_row
    blocks = 4
    per_block = -(-units // (total * blocks))
    rows = tok // blocks

    def make_unit(u):
        band = u // per_row
        left = lax.rem(u, per_row) * run_cols
        base = base_ref[band // (RANK // STEP)] + lax.rem(band, RANK // STEP) * (STEP * cols) + left
        for j in range(4):
            table[
                span(band * STEP, STEP), pl.ds(pl.multiple_of(left + j * WIDE, WIDE), WIDE)
            ] = signs(local + (base + j * WIDE))

    head_jobs = []
    for i in range(SLOTS):
        head_jobs += [(3 + i, job1, i), (5 + i, job2, i), (7 + i, job3, i)]
    head_jobs.sort(key=lambda item: item[0])
    head_late = [(i, job0, i) for i in range(SLOTS)]
    head_late += [(total - SLOTS + i, job0, SLOTS + i) for i in range(SLOTS)]

    def head(c, carry):
        run(head_jobs, c)
        slot = lax.rem(c, SLOTS)
        loaded(in_ref, 0, slot).wait()
        which = c // chunks

        def block(i, inner):
            where = span(i * rows, rows)
            away[c, where, :] = jnp.dot(
                wide[slot, 1 - x, where, :], weights[which], preferred_element_type=jnp.float32
            ).astype(jnp.bfloat16)
            keep[c, where, :] = jnp.dot(
                wide[slot, x, where, :], weights[which], preferred_element_type=jnp.float32
            )
            for j in range(per_block):
                make_unit(lax.rem((c * blocks + i) * per_block + j, units))
            return inner

        lax.fori_loop(0, blocks, block, 0)
        run(head_late, c)
        ahead = c + SLOTS

        @pl.when(ahead < chunks)
        def _():
            loaded(in_ref, ahead, slot).start()

        @pl.when((ahead >= chunks) & (ahead < total))
        def _():
            loaded(gr_ref, ahead - chunks, slot).start()

        @pl.when(ahead >= total)
        def _():
            loaded(gr_ref, ahead - total, slot).start()

        return carry

    lax.fori_loop(0, total, head, 0)

    def grads(phase, group):
        mean, var = ((mean_r_ref, var_r_ref), (mean_t, var_t))[phase]

        def sample(i, carry):
            grad = lax.dot_general(
                low[phase, span((group * GROUP + i) * tok, tok), :],
                wide[i // PAIR, lax.rem(i, PAIR)],
                (((0,), (0,)), ((), ())), preferred_element_type=jnp.float32,
            )
            step[span(i * RANK, RANK), :] = (
                (0.9 * mean[...] + 0.1 * grad)
                * lax.rsqrt(0.999 * var[...] + 0.001 * grad * grad)
            ).astype(jnp.bfloat16)
            return carry

        lax.fori_loop(0, GROUP, sample, 0)

    fresh = w // groups

    def project(phase, group, jobs):
        row0 = phase * down_row
        side0 = w + phase * RANK

        def tile(k, carry):
            run(jobs, k)
            col = pl.ds(pl.multiple_of(k * TILE, TILE), TILE)
            mixed = jnp.dot(
                step[...], table[row0 : row0 + w, col], preferred_element_type=jnp.float32
            )
            side = table[side0 : side0 + RANK, col].astype(jnp.float32)
            for i in range(GROUP):
                line = jnp.sum(mixed[i * RANK : (i + 1) * RANK] * side, axis=0, keepdims=True)
                width = min(w, TILE)
                for s in range(TILE // width):
                    if w >= TILE:
                        shard = k // (w // TILE)
                        lanes = pl.ds(pl.multiple_of(lax.rem(k, w // TILE) * TILE, TILE), TILE)
                    else:
                        shard, lanes = k * (TILE // width) + s, pl.ds(0, width)
                    part = line[:, s * width : (s + 1) * width]
                    if phase == 0:
                        acc[group, shard, i : i + 1, lanes] = part
                    else:
                        acc[group, shard, i : i + 1, lanes] = (
                            acc[group, shard, i : i + 1, lanes] + part
                        )
            if phase == 0:
                for r in range(group * fresh, (group + 1) * fresh, STEP):
                    base = base_ref[(down_row + r) // RANK] + ((r % RANK) * cols + k * TILE)
                    table[down_row + r : down_row + r + STEP, col] = signs(local + base)
            return carry

        lax.fori_loop(0, cols // TILE, tile, 0)

    def shared(group, d):
        target = lax.rem(me + d, shards)
        s = group * (shards - 1) + d - 1
        return remote(acc.at[group, target], pieces.at[group, d - 1], ps.at[s], pr.at[s], target)

    ticks = cols // TILE
    at = lambda quarter: ticks * quarter // 16
    passes = [(phase, group) for phase in range(2) for group in range(groups)]
    for index, (phase, group) in enumerate(passes):
        for i in range(SLOTS):
            job4(index * SLOTS + i)
        for slot in range(SLOTS):
            loaded(in_ref, 0, slot).wait()
        grads(phase, group)
        jobs = []
        if index + 1 < len(passes):
            after = passes[index + 1]
            for slot in range(SLOTS):
                loaded((gr_ref, in_ref)[after[0]], after[1] * SLOTS + slot, slot).start()
            for i in range(SLOTS):
                c = (index + 1) * SLOTS + i
                jobs += [(at(0 + 2 * i), job1, c), (at(4 + 2 * i), job2, c), (at(8 + 2 * i), job3, c)]
                if c + SLOTS < total:
                    jobs.append((at(11 + 2 * i), job0, c + SLOTS))
            jobs.sort(key=lambda item: item[0])
        project(phase, group, jobs)
        if phase == 1:
            for d in range(1, shards):
                shared(group, d).start()

    for group in range(groups):
        for d in range(1, shards):
            shared(group, d).wait_recv()
        raw = acc[group, me]
        for d in range(1, shards):
            raw = raw + pieces[group, d - 1]
        raw_ref[group] = raw
    for c in range(total):
        first(c).wait_send()
        fourth(c).wait_send()
        for d in range(1, rest):
            second(c, d).wait_send()
            third(c, d).wait_send()
    for group in range(groups):
        for d in range(1, shards):
            shared(group, d).wait_send()


def main(bases, left, right, mean_l, var_l, mean_r, var_r, wide_in, wide_gr, shards, cols):
    n, tok, w = wide_in.shape
    rest = shards // 2
    groups = n // GROUP
    total = 2 * n // PAIR
    vmem = pl.BlockSpec(memory_space=pltpu.VMEM)
    hbm = pl.BlockSpec(memory_space=pl.ANY)
    dma = pltpu.SemaphoreType.DMA
    few, many = dma((total,)), dma((total * (rest - 1),))
    return pl.pallas_call(
        functools.partial(main_kernel, shards, cols),
        in_specs=[pl.BlockSpec(memory_space=pltpu.SMEM)] + [vmem] * 6 + [hbm] * 2,
        out_specs=vmem,
        out_shape=jax.ShapeDtypeStruct((groups, GROUP, w), jnp.float32),
        scratch_shapes=[
            pltpu.VMEM((2 * w + 2 * RANK, cols), jnp.bfloat16),
            pltpu.VMEM((SLOTS, PAIR, tok, w), jnp.bfloat16),
            pltpu.VMEM((2, w, RANK), jnp.bfloat16),
            pltpu.VMEM((RANK, w), jnp.float32),
            pltpu.VMEM((RANK, w), jnp.float32),
            pltpu.VMEM((total, tok, RANK), jnp.float32),
            pltpu.VMEM((total, tok, RANK), jnp.bfloat16),
            pltpu.VMEM((total, tok, RANK), jnp.bfloat16),
            pltpu.VMEM((total, tok, RANK), jnp.bfloat16),
            pltpu.VMEM((total * (rest - 1), tok // rest, RANK), jnp.bfloat16),
            pltpu.VMEM((2, n * tok, RANK), jnp.bfloat16),
            pltpu.VMEM((GROUP * RANK, w), jnp.bfloat16),
            pltpu.VMEM((groups, shards, GROUP, w), jnp.float32),
            pltpu.VMEM((groups, shards - 1, GROUP, w), jnp.float32),
            dma((SLOTS,)), few, few, many, many, many, many, few, few,
            dma((groups * (shards - 1),)), dma((groups * (shards - 1),)),
        ],
        compiler_params=pltpu.CompilerParams(
            collective_id=1, has_side_effects=True, vmem_limit_bytes=63 * 1024 * 1024
        ),
        cost_estimate=pl.CostEstimate(
            flops=4 * n * RANK * w * cols, bytes_accessed=8 * n * tok * w, transcendentals=0
        ),
        name="main",
    )(bases, left, right, mean_l, var_l, mean_r, var_r, wide_in, wide_gr)


def finish_kernel(
    shards, langs, nval,
    raw_ref, val_ref, hot_ref, count_ref,
    feat_ref, score_ref,
    message, notes, send, recv,
):
    me = lax.axis_index("proj")
    n, w = feat_ref.shape
    cols = shards * w
    barrier = pltpu.get_barrier_semaphore()
    for d in range(1, shards):
        pl.semaphore_signal(
            barrier, inc=1, device_id={"proj": lax.rem(me + d, shards)}, device_id_type=MESH
        )

    raw = jnp.concatenate([raw_ref[g] for g in range(raw_ref.shape[0])], axis=0)
    raw_low = raw.astype(jnp.bfloat16)
    ones = jnp.ones((16, w), jnp.bfloat16)
    both = (((1,), (1,)), ((), ()))
    own = jnp.zeros((n, nval), jnp.float32)
    square = jnp.zeros((n, nval), jnp.float32)
    for l in range(langs):
        val = val_ref[l * nval : (l + 1) * nval, :]
        hot = hot_ref[:, l : l + 1]
        own = own + hot * lax.dot_general(raw_low, val, both, preferred_element_type=jnp.float32)
        wide = val.astype(jnp.float32)
        sums = lax.dot_general(
            ones, (wide * wide).astype(jnp.bfloat16), both, preferred_element_type=jnp.float32
        )
        square = square + hot * sums[0:1]
    message[...] = jnp.zeros(message.shape, jnp.bfloat16)
    message[16 : 16 + n, :nval] = square.astype(jnp.bfloat16)
    message[:n, :nval] = own.astype(jnp.bfloat16)
    message[:n, nval:] = jnp.broadcast_to(
        jnp.sum(raw * raw, axis=1, keepdims=True), (n, message.shape[1] - nval)
    ).astype(jnp.bfloat16)
    pl.semaphore_wait(barrier, shards - 1)
    copies = []
    for d in range(1, shards):
        target = lax.rem(me + d, shards)
        copy = pltpu.make_async_remote_copy(
            src_ref=message, dst_ref=notes.at[d - 1],
            send_sem=send.at[d - 1], recv_sem=recv.at[d - 1],
            device_id={"proj": target}, device_id_type=MESH,
        )
        copy.start()
        copies.append(copy)
    total = message[...].astype(jnp.float32)
    for copy in copies:
        copy.wait_recv()
    for d in range(1, shards):
        total = total + notes[d - 1].astype(jnp.float32)
    inverse = lax.rsqrt(total[:n, nval : nval + 1] / cols + 1e-06)
    feat_ref[...] = raw * inverse
    rms = jnp.sqrt(total[16 : 16 + n, :nval] / cols + 1e-06)
    similar = total[:n, :nval] * inverse / (math.sqrt(cols) * rms)
    live = lax.broadcasted_iota(jnp.int32, (n, nval), 1) < count_ref[...]
    best = jnp.max(jnp.where(live, similar, jnp.float32(-1e30)), axis=1, keepdims=True)
    score_ref[...] = jnp.broadcast_to(best, score_ref.shape)
    for copy in copies:
        copy.wait_send()


def finish(raw, all_val, hot, count, shards):
    groups, size, w = raw.shape
    n = groups * size
    langs, nval = all_val.shape[0], all_val.shape[1]
    vmem = pl.BlockSpec(memory_space=pltpu.VMEM)
    return pl.pallas_call(
        functools.partial(finish_kernel, shards, langs, nval),
        in_specs=[vmem] * 4,
        out_specs=[vmem] * 2,
        out_shape=[
            jax.ShapeDtypeStruct((n, w), jnp.float32),
            jax.ShapeDtypeStruct((n, 128), jnp.float32),
        ],
        scratch_shapes=[
            pltpu.VMEM((32, nval + 128), jnp.bfloat16),
            pltpu.VMEM((shards - 1, 32, nval + 128), jnp.bfloat16),
            pltpu.SemaphoreType.DMA((shards - 1,)),
            pltpu.SemaphoreType.DMA((shards - 1,)),
        ],
        compiler_params=pltpu.CompilerParams(
            collective_id=0, has_side_effects=True, vmem_limit_bytes=32 * 1024 * 1024
        ),
        name="finish",
    )(raw, all_val.reshape(langs * nval, w), hot, count)


def per_device(
    mapped_layer_arguments,
    loss_slope_at_result,
    left_lowrank_weights,
    right_lowrank_weights,
    mean_estimate_left,
    variance_estimate_left,
    mean_estimate_right,
    variance_estimate_right,
    heldout_sketched_slopes,
    tongue_label_per_example,
    heldout_example_tally,
    sketch_random_key,
):
    shard_id = lax.axis_index("proj")
    shards = lax.axis_size("proj")
    n, tok, w = mapped_layer_arguments.shape
    K = w * shards

    seed4 = sketch_random_key[0] * 4
    inner = jnp.arange(w // RANK, dtype=jnp.int32) * (RANK * K) + shard_id * (w * K)
    bases = jnp.concatenate([
        scramble(seed4 + 1) + inner,
        scramble(seed4)[None],
        scramble(seed4 + 3)[None],
        scramble(seed4 + 2) + inner,
    ])
    raw = main(
        bases, left_lowrank_weights, right_lowrank_weights, mean_estimate_left,
        variance_estimate_left, mean_estimate_right, variance_estimate_right,
        mapped_layer_arguments, loss_slope_at_result, shards, K,
    )

    all_val = lax.all_gather(heldout_sketched_slopes, "lang", axis=0, tiled=True)
    lang_of = tongue_label_per_example[:, 0]
    num_langs = heldout_example_tally.shape[0]
    hot = (lang_of[:, None] == lax.iota(jnp.int32, num_langs)[None, :]).astype(jnp.float32)
    count_own = jnp.sum(
        hot.astype(jnp.int32) * heldout_example_tally[None, :], axis=1, keepdims=True
    )
    features, scores = finish(raw, all_val, hot, count_own, shards)
    scores = scores[:, 0]
    return (features, scores)


def solution(mesh):
    in_specs = (
        P("lang", None, "proj"),
        P("lang", None, "proj"),
        P("proj", None),
        P(None, "proj"),
        P("proj", None),
        P("proj", None),
        P(None, "proj"),
        P(None, "proj"),
        P("lang", None, "proj"),
        P("lang", None),
        P(),
        P(),
    )
    out_specs = (P("lang", "proj"), P("lang"))
    return jax.shard_map(
        per_device, mesh=mesh, in_specs=in_specs, out_specs=out_specs, check_vma=False
    )
```

```python
import functools
import math

import jax
import jax.numpy as jnp
from jax import lax
from jax.experimental import pallas as pl
from jax.experimental.pallas import tpu as pltpu
from jax.sharding import PartitionSpec as P

RANK = 128
UPDATE_MULTIPLIER = 1.25
M1 = 2146121005
M2_UP = (739982445 * 4 + 2**31) % 2**32 - 2**31
MESH = pl.DeviceIdType.MESH

PAIR = 2
SLOTS = 3
GROUP = PAIR * SLOTS
STEP, WIDE = 16, 512
TILE = 1024


def scramble(hashed):
    hashed = jnp.bitwise_xor(hashed, lax.shift_right_logical(hashed, jnp.int32(16)))
    hashed = hashed * 2146121005
    hashed = jnp.bitwise_xor(hashed, lax.shift_right_logical(hashed, jnp.int32(15)))
    hashed = hashed * 739982445
    hashed = jnp.bitwise_xor(hashed, lax.shift_right_logical(hashed, jnp.int32(16)))
    return hashed


def signs(h):
    h = h ^ lax.shift_right_logical(h, jnp.int32(16))
    h = h * jnp.int32(M1)
    h = h ^ lax.shift_right_logical(h, jnp.int32(15))
    h = h * jnp.int32(M2_UP)
    h = h ^ lax.shift_left(h, jnp.int32(16))
    return jnp.where(h < 0, jnp.float32(-1.0), jnp.float32(1.0)).astype(jnp.bfloat16)


HOP, DELAY, MARGIN, BACKLOG, FLYING = 2.5, 0.5, 0.0, 3.0, 4
HEAD_TICK, GRADS, TICK = 2.0, 2.5, 1.9


def plan(total, passes, ticks):
    arrived, started, free = {}, [0] * total, [0.0, 0.0]
    now, head, ready, beside = 0.0, [], [], []

    def due():
        jobs = []
        for stage in (3, 2, 1, 0):
            link = (0, 1, 1, 0)[stage]
            for c in range(total):
                if started[c] != stage or free[link] - now > BACKLOG:
                    continue
                if stage == 0:
                    flying = sum(0 < s < 4 for s in started)
                    if HEAD_TICK * (c + 1) > now + 0.01 or flying >= FLYING:
                        continue
                elif arrived[c, stage - 1] + MARGIN > now:
                    continue
                free[link] = max(free[link], now) + HOP
                arrived[c, stage] = free[link] + DELAY
                started[c] = stage + 1
                jobs.append((stage, c))
        return jobs

    for c in range(total):
        head += [(c,) + job for job in due()]
        now += HEAD_TICK
    for index in range(passes):
        need = range(index * total // passes, (index + 1) * total // passes)
        while any(started[c] < 4 for c in need):
            ready += [(index,) + job for job in due()]
            now += 0.5
        ready += [(index, 4, c) for c in need]
        now = max([now] + [arrived[c, 3] for c in need]) + GRADS
        for k in range(ticks):
            beside += [(index * ticks + k,) + job for job in due()]
            now += TICK
    return head, ready, beside


def main_kernel(
    shards, cols,
    base_ref, left_ref, right_ref, mean_l_ref, var_l_ref, mean_r_ref, var_r_ref, in_ref, gr_ref,
    raw_ref,
    table, wide, weights, means, variances, keep, away, pair, land, low, step, acc, pieces,
    load, held, xs, xr, zs, zr, gs, gr, ys, yr, ps, pr,
):
    me = lax.axis_index("proj")
    rest = shards // 2
    x, z = lax.rem(me, 2), me // 2
    n, tok, w = in_ref.shape
    chunks = n // PAIR
    total = 2 * chunks
    groups = n // GROUP
    piece = tok // rest
    partner = z * 2 + (1 - x)
    others = [lax.rem(z + d, rest) for d in range(1, rest)]
    down_row = w + 2 * RANK

    def span(start, size):
        return pl.ds(pl.multiple_of(start, 16), size)

    def loaded(source, c, slot):
        return pltpu.make_async_copy(
            source.at[pl.ds(c * PAIR, PAIR)], wide.at[slot], load.at[slot]
        )

    for c in range(SLOTS):
        loaded(in_ref, c, c).start()

    part = w // 2
    moments = [
        pltpu.make_async_copy(mean_r_ref, means.at[0], held.at[0]),
        pltpu.make_async_copy(var_r_ref, variances.at[0], held.at[1]),
    ] + [
        pltpu.make_async_copy(
            (mean_l_ref, var_l_ref)[i // 2].at[pl.ds((i % 2) * part, part)],
            keep.at[total - 4 + i, pl.ds(0, part)], held.at[2 + i],
        )
        for i in range(4)
    ]
    for copy in moments:
        copy.start()

    barrier = pltpu.get_barrier_semaphore()
    for d in range(1, shards):
        pl.semaphore_signal(
            barrier, inc=1, device_id={"proj": lax.rem(me + d, shards)}, device_id_type=MESH
        )

    weights[0] = left_ref[...]
    weights[1] = right_ref[...].astype(jnp.float32).T.astype(jnp.bfloat16)
    pl.semaphore_wait(barrier, shards - 1)

    def remote(src, dst, send, recv, target):
        return pltpu.make_async_remote_copy(
            src_ref=src, dst_ref=dst, send_sem=send, recv_sem=recv,
            device_id={"proj": target}, device_id_type=MESH,
        )

    def first(c):
        return remote(away.at[c], pair.at[c], xs.at[c], xr.at[c], partner)

    def second(c, d):
        s = c * (rest - 1) + d - 1
        return remote(
            away.at[c, span(others[d - 1] * piece, piece)], land.at[s],
            zs.at[s], zr.at[s], others[d - 1] * 2 + x,
        )

    def third(c, d):
        s = c * (rest - 1) + d - 1
        where = span((c % chunks) * PAIR * tok + x * tok + z * piece, piece)
        return remote(
            low.at[c // chunks, where], low.at[c // chunks, where],
            gs.at[s], gr.at[s], others[d - 1] * 2 + x,
        )

    def fourth(c):
        where = span((c % chunks) * PAIR * tok + x * tok, tok)
        return remote(
            low.at[c // chunks, where], low.at[c // chunks, where], ys.at[c], yr.at[c], partner
        )

    def job0(c):
        first(c).start()

    def job1(c):
        first(c).wait_recv()
        first(c).wait_send()
        away[c] = (keep[c] + pair[c].astype(jnp.float32)).astype(jnp.bfloat16)
        for d in range(1, rest):
            second(c, d).start()

    def job2(c):
        for d in range(1, rest):
            second(c, d).wait_recv()
        summed = away[c, span(z * piece, piece), :].astype(jnp.float32)
        for d in range(1, rest):
            summed = summed + land[c * (rest - 1) + d - 1].astype(jnp.float32)
        where = span((c % chunks) * PAIR * tok + x * tok + z * piece, piece)
        low[c // chunks, where, :] = (UPDATE_MULTIPLIER * summed).astype(jnp.bfloat16)
        for d in range(1, rest):
            third(c, d).start()

    def job3(c):
        for d in range(1, rest):
            third(c, d).wait_recv()
        fourth(c).start()

    def job4(c):
        fourth(c).wait_recv()

    def run(jobs, tick):
        for when in sorted(set(job[0] for job in jobs)):
            @pl.when(tick == when)
            def _():
                for _, stage, c in [job for job in jobs if job[0] == when]:
                    (job0, job1, job2, job3, job4)[stage](c)

    local = lax.broadcasted_iota(jnp.int32, (STEP, WIDE), 0) * cols + lax.broadcasted_iota(
        jnp.int32, (STEP, WIDE), 1
    )
    run_cols = 4 * WIDE
    per_row = cols // run_cols
    units = ((w + RANK) // STEP) * per_row
    per_chunk = -(-units // total)

    def make_unit(u):
        band = u // per_row
        left = lax.rem(u, per_row) * run_cols
        base = base_ref[band // (RANK // STEP)] + lax.rem(band, RANK // STEP) * (STEP * cols) + left
        for j in range(4):
            table[
                span(band * STEP, STEP), pl.ds(pl.multiple_of(left + j * WIDE, WIDE), WIDE)
            ] = signs(local + (base + j * WIDE))

    ticks = cols // TILE
    head_jobs, ready_jobs, pass_jobs = plan(total, 2 * groups, ticks)

    def head(c, carry):
        run(head_jobs, c)

        @pl.when(c == total // 2)
        def _():
            for copy in moments:
                copy.wait()
            for i in range(4):
                (means, variances)[i // 2][1, :, (i % 2) * part : (i % 2 + 1) * part] = keep[
                    total - 4 + i, 0:part, :
                ].T

        slot = lax.rem(c, SLOTS)
        loaded(in_ref, 0, slot).wait()
        which = c // chunks

        away[c] = jnp.dot(
            wide[slot, 1 - x], weights[which], preferred_element_type=jnp.float32
        ).astype(jnp.bfloat16)
        keep[c] = jnp.dot(wide[slot, x], weights[which], preferred_element_type=jnp.float32)
        for j in range(per_chunk):
            make_unit(lax.rem(c * per_chunk + j, units))
        ahead = c + SLOTS

        @pl.when(ahead < chunks)
        def _():
            loaded(in_ref, ahead, slot).start()

        @pl.when((ahead >= chunks) & (ahead < total))
        def _():
            loaded(gr_ref, ahead - chunks, slot).start()

        @pl.when(ahead >= total)
        def _():
            loaded(gr_ref, ahead - total, slot).start()

        return carry

    lax.fori_loop(0, total, head, 0)

    def grads(phase, group):
        mean, var = means.at[phase], variances.at[phase]

        def sample(i, carry):
            grad = lax.dot_general(
                low[phase, span((group * GROUP + i) * tok, tok), :],
                wide[i // PAIR, lax.rem(i, PAIR)],
                (((0,), (0,)), ((), ())), preferred_element_type=jnp.float32,
            )
            step[span(i * RANK, RANK), :] = (
                (0.9 * mean[...] + 0.1 * grad)
                * lax.rsqrt(0.999 * var[...] + 0.001 * grad * grad)
            ).astype(jnp.bfloat16)
            return carry

        lax.fori_loop(0, GROUP, sample, 0)

    fresh_row = w + RANK
    fresh = (w + RANK) // groups
    width = min(w, TILE)
    near = lax.broadcasted_iota(jnp.int32, (STEP, TILE), 0) * cols + lax.broadcasted_iota(
        jnp.int32, (STEP, TILE), 1
    )

    def project(phase, group):
        row0 = phase * down_row
        side0 = w + phase * RANK

        def tile(k, carry):
            run(pass_jobs, (phase * groups + group) * ticks + k)
            col = pl.ds(pl.multiple_of(k * TILE, TILE), TILE)
            mixed = jnp.dot(
                step[...], table[row0 : row0 + w, col], preferred_element_type=jnp.float32
            )
            side = table[side0 : side0 + RANK, col].astype(jnp.float32)
            for i in range(GROUP):
                line = jnp.sum(mixed[i * RANK : (i + 1) * RANK] * side, axis=0, keepdims=True)
                for s in range(TILE // width):
                    if w >= TILE:
                        shard = k // (w // TILE)
                        lanes = pl.ds(pl.multiple_of(lax.rem(k, w // TILE) * TILE, TILE), TILE)
                    else:
                        shard, lanes = k * (TILE // width) + s, pl.ds(0, width)
                    part = line[:, s * width : (s + 1) * width]
                    if phase == 0:
                        acc[group, shard, i : i + 1, lanes] = part
                    else:
                        acc[group, shard, i : i + 1, lanes] = (
                            acc[group, shard, i : i + 1, lanes] + part
                        )
            if phase == 0:
                for r in range(0, fresh, STEP):
                    row = fresh_row + group * fresh + r
                    base = base_ref[row // RANK] + (lax.rem(row, RANK) * cols + k * TILE)
                    table[span(row, STEP), col] = signs(near + base)
            return carry

        lax.fori_loop(0, ticks, tile, 0)

    def shared(group, d):
        target = lax.rem(me + d, shards)
        s = group * (shards - 1) + d - 1
        return remote(acc.at[group, target], pieces.at[group, d - 1], ps.at[s], pr.at[s], target)

    for phase in range(2):
        source = (gr_ref, in_ref)[phase]

        def one_pass(group, carry):
            run(ready_jobs, phase * groups + group)
            for slot in range(SLOTS):
                loaded(source, 0, slot).wait()
            grads(phase, group)

            @pl.when(group + 1 < groups)
            def _():
                for slot in range(SLOTS):
                    loaded(source, (group + 1) * SLOTS + slot, slot).start()

            if phase == 0:
                @pl.when(group + 1 == groups)
                def _():
                    for slot in range(SLOTS):
                        loaded(in_ref, slot, slot).start()

            project(phase, group)
            if phase == 1:
                for d in range(1, shards):
                    shared(group, d).start()
            return carry

        lax.fori_loop(0, groups, one_pass, 0)

    for group in range(groups):
        for d in range(1, shards):
            shared(group, d).wait_recv()
        raw = acc[group, me]
        for d in range(1, shards):
            raw = raw + pieces[group, d - 1]
        raw_ref[group] = raw
    for c in range(total):
        fourth(c).wait_send()
        for d in range(1, rest):
            second(c, d).wait_send()
            third(c, d).wait_send()
    for group in range(groups):
        for d in range(1, shards):
            shared(group, d).wait_send()


def main(bases, left, right, mean_l, var_l, mean_r, var_r, wide_in, wide_gr, shards, cols):
    n, tok, w = wide_in.shape
    rest = shards // 2
    groups = n // GROUP
    total = 2 * n // PAIR
    vmem = pl.BlockSpec(memory_space=pltpu.VMEM)
    hbm = pl.BlockSpec(memory_space=pl.ANY)
    dma = pltpu.SemaphoreType.DMA
    few, many = dma((total,)), dma((total * (rest - 1),))
    return pl.pallas_call(
        functools.partial(main_kernel, shards, cols),
        in_specs=[pl.BlockSpec(memory_space=pltpu.SMEM)] + [vmem] * 2 + [hbm] * 6,
        out_specs=vmem,
        out_shape=jax.ShapeDtypeStruct((groups, GROUP, w), jnp.float32),
        scratch_shapes=[
            pltpu.VMEM((2 * w + 2 * RANK, cols), jnp.bfloat16),
            pltpu.VMEM((SLOTS, PAIR, tok, w), jnp.bfloat16),
            pltpu.VMEM((2, w, RANK), jnp.bfloat16),
            pltpu.VMEM((2, RANK, w), jnp.float32),
            pltpu.VMEM((2, RANK, w), jnp.float32),
            pltpu.VMEM((total, tok, RANK), jnp.float32),
            pltpu.VMEM((total, tok, RANK), jnp.bfloat16),
            pltpu.VMEM((total, tok, RANK), jnp.bfloat16),
            pltpu.VMEM((total * (rest - 1), tok // rest, RANK), jnp.bfloat16),
            pltpu.VMEM((2, n * tok, RANK), jnp.bfloat16),
            pltpu.VMEM((GROUP * RANK, w), jnp.bfloat16),
            pltpu.VMEM((groups, shards, GROUP, w), jnp.float32),
            pltpu.VMEM((groups, shards - 1, GROUP, w), jnp.float32),
            dma((SLOTS,)), dma((6,)), few, few, many, many, many, many, few, few,
            dma((groups * (shards - 1),)), dma((groups * (shards - 1),)),
        ],
        compiler_params=pltpu.CompilerParams(
            collective_id=1, has_side_effects=True, vmem_limit_bytes=63 * 1024 * 1024
        ),
        cost_estimate=pl.CostEstimate(
            flops=4 * n * RANK * w * cols, bytes_accessed=8 * n * tok * w, transcendentals=0
        ),
        name="main",
    )(bases, left, right, mean_l, var_l, mean_r, var_r, wide_in, wide_gr)


def finish_kernel(
    shards, langs, nval,
    raw_ref, val_ref, hot_ref, count_ref,
    feat_ref, score_ref,
    message, notes, send, recv,
):
    me = lax.axis_index("proj")
    n, w = feat_ref.shape
    cols = shards * w
    barrier = pltpu.get_barrier_semaphore()
    for d in range(1, shards):
        pl.semaphore_signal(
            barrier, inc=1, device_id={"proj": lax.rem(me + d, shards)}, device_id_type=MESH
        )

    raw = jnp.concatenate([raw_ref[g] for g in range(raw_ref.shape[0])], axis=0)
    raw_low = raw.astype(jnp.bfloat16)
    ones = jnp.ones((16, w), jnp.bfloat16)
    both = (((1,), (1,)), ((), ()))
    own = jnp.zeros((n, nval), jnp.float32)
    square = jnp.zeros((n, nval), jnp.float32)
    for l in range(langs):
        val = val_ref[l * nval : (l + 1) * nval, :]
        hot = hot_ref[:, l : l + 1]
        own = own + hot * lax.dot_general(raw_low, val, both, preferred_element_type=jnp.float32)
        wide = val.astype(jnp.float32)
        sums = lax.dot_general(
            ones, (wide * wide).astype(jnp.bfloat16), both, preferred_element_type=jnp.float32
        )
        square = square + hot * sums[0:1]
    message[...] = jnp.zeros(message.shape, jnp.bfloat16)
    message[16 : 16 + n, :nval] = square.astype(jnp.bfloat16)
    message[:n, :nval] = own.astype(jnp.bfloat16)
    message[:n, nval:] = jnp.broadcast_to(
        jnp.sum(raw * raw, axis=1, keepdims=True), (n, message.shape[1] - nval)
    ).astype(jnp.bfloat16)
    pl.semaphore_wait(barrier, shards - 1)
    copies = []
    for d in range(1, shards):
        target = lax.rem(me + d, shards)
        copy = pltpu.make_async_remote_copy(
            src_ref=message, dst_ref=notes.at[d - 1],
            send_sem=send.at[d - 1], recv_sem=recv.at[d - 1],
            device_id={"proj": target}, device_id_type=MESH,
        )
        copy.start()
        copies.append(copy)
    total = message[...].astype(jnp.float32)
    for copy in copies:
        copy.wait_recv()
    for d in range(1, shards):
        total = total + notes[d - 1].astype(jnp.float32)
    inverse = lax.rsqrt(total[:n, nval : nval + 1] / cols + 1e-06)
    feat_ref[...] = raw * inverse
    rms = jnp.sqrt(total[16 : 16 + n, :nval] / cols + 1e-06)
    similar = total[:n, :nval] * inverse / (math.sqrt(cols) * rms)
    live = lax.broadcasted_iota(jnp.int32, (n, nval), 1) < count_ref[...]
    best = jnp.max(jnp.where(live, similar, jnp.float32(-1e30)), axis=1, keepdims=True)
    score_ref[...] = jnp.broadcast_to(best, score_ref.shape)
    for copy in copies:
        copy.wait_send()


def finish(raw, all_val, hot, count, shards):
    groups, size, w = raw.shape
    n = groups * size
    langs, nval = all_val.shape[0], all_val.shape[1]
    vmem = pl.BlockSpec(memory_space=pltpu.VMEM)
    return pl.pallas_call(
        functools.partial(finish_kernel, shards, langs, nval),
        in_specs=[vmem] * 4,
        out_specs=[vmem] * 2,
        out_shape=[
            jax.ShapeDtypeStruct((n, w), jnp.float32),
            jax.ShapeDtypeStruct((n, 128), jnp.float32),
        ],
        scratch_shapes=[
            pltpu.VMEM((32, nval + 128), jnp.bfloat16),
            pltpu.VMEM((shards - 1, 32, nval + 128), jnp.bfloat16),
            pltpu.SemaphoreType.DMA((shards - 1,)),
            pltpu.SemaphoreType.DMA((shards - 1,)),
        ],
        compiler_params=pltpu.CompilerParams(
            collective_id=0, has_side_effects=True, vmem_limit_bytes=32 * 1024 * 1024
        ),
        name="finish",
    )(raw, all_val.reshape(langs * nval, w), hot, count)


def per_device(
    mapped_layer_arguments,
    loss_slope_at_result,
    left_lowrank_weights,
    right_lowrank_weights,
    mean_estimate_left,
    variance_estimate_left,
    mean_estimate_right,
    variance_estimate_right,
    heldout_sketched_slopes,
    tongue_label_per_example,
    heldout_example_tally,
    sketch_random_key,
):
    shard_id = lax.axis_index("proj")
    shards = lax.axis_size("proj")
    n, tok, w = mapped_layer_arguments.shape
    K = w * shards

    seed4 = sketch_random_key[0] * 4
    inner = jnp.arange(w // RANK, dtype=jnp.int32) * (RANK * K) + shard_id * (w * K)
    bases = jnp.concatenate([
        scramble(seed4 + 1) + inner,
        scramble(seed4)[None],
        scramble(seed4 + 3)[None],
        scramble(seed4 + 2) + inner,
    ])
    raw = main(
        bases, left_lowrank_weights, right_lowrank_weights, mean_estimate_left,
        variance_estimate_left, mean_estimate_right, variance_estimate_right,
        mapped_layer_arguments, loss_slope_at_result, shards, K,
    )

    all_val = lax.all_gather(heldout_sketched_slopes, "lang", axis=0, tiled=True)
    lang_of = tongue_label_per_example[:, 0]
    num_langs = heldout_example_tally.shape[0]
    hot = (lang_of[:, None] == lax.iota(jnp.int32, num_langs)[None, :]).astype(jnp.float32)
    count_own = jnp.sum(
        hot.astype(jnp.int32) * heldout_example_tally[None, :], axis=1, keepdims=True
    )
    features, scores = finish(raw, all_val, hot, count_own, shards)
    scores = scores[:, 0]
    return (features, scores)


def solution(mesh):
    in_specs = (
        P("lang", None, "proj"),
        P("lang", None, "proj"),
        P("proj", None),
        P(None, "proj"),
        P("proj", None),
        P("proj", None),
        P(None, "proj"),
        P(None, "proj"),
        P("lang", None, "proj"),
        P("lang", None),
        P(),
        P(),
    )
    out_specs = (P("lang", "proj"), P("lang"))
    return jax.shard_map(
        per_device, mesh=mesh, in_specs=in_specs, out_specs=out_specs, check_vma=False
    )
```

```python
import functools
import math

import jax
import jax.numpy as jnp
from jax import lax
from jax.experimental import pallas as pl
from jax.experimental.pallas import tpu as pltpu
from jax.sharding import PartitionSpec as P

RANK = 128
UPDATE_MULTIPLIER = 1.25
M1 = 2146121005
M2_UP = (739982445 * 4 + 2**31) % 2**32 - 2**31
MESH = pl.DeviceIdType.MESH

PAIR = 2
SLOTS = 3
GROUP = PAIR * SLOTS
STEP, WIDE = 16, 512
TILE = 1024


def scramble(hashed):
    hashed = jnp.bitwise_xor(hashed, lax.shift_right_logical(hashed, jnp.int32(16)))
    hashed = hashed * 2146121005
    hashed = jnp.bitwise_xor(hashed, lax.shift_right_logical(hashed, jnp.int32(15)))
    hashed = hashed * 739982445
    hashed = jnp.bitwise_xor(hashed, lax.shift_right_logical(hashed, jnp.int32(16)))
    return hashed


def signs(h):
    h = h ^ lax.shift_right_logical(h, jnp.int32(16))
    h = h * jnp.int32(M1)
    h = h ^ lax.shift_right_logical(h, jnp.int32(15))
    h = h * jnp.int32(M2_UP)
    h = h ^ lax.shift_left(h, jnp.int32(16))
    return jnp.where(h < 0, jnp.float32(-1.0), jnp.float32(1.0)).astype(jnp.bfloat16)


HOP, DELAY, MARGIN, BACKLOG, FLYING = 3.0, 0.3, 0.0, 5.0, 4
HEAD_TICK, GRADS, TICK = 2.5, 2.5, 2.1


def plan(total, passes, ticks):
    arrived, started, free = {}, [0] * total, [0.0, 0.0]
    now, head, ready, beside = 0.0, [], [], []

    def due():
        jobs = []
        for stage in (3, 2, 1, 0):
            link = (0, 1, 1, 0)[stage]
            for c in range(total):
                if started[c] != stage or free[link] - now > BACKLOG:
                    continue
                if stage == 0:
                    flying = sum(0 < s < 4 for s in started)
                    if HEAD_TICK * (c + 1) > now + 0.01 or flying >= FLYING:
                        continue
                elif arrived[c, stage - 1] + MARGIN > now:
                    continue
                free[link] = max(free[link], now) + HOP
                arrived[c, stage] = free[link] + DELAY
                started[c] = stage + 1
                jobs.append((stage, c))
        return jobs

    for c in range(total):
        head += [(c,) + job for job in due()]
        now += HEAD_TICK
    for index in range(passes):
        need = range(index * total // passes, (index + 1) * total // passes)
        while any(started[c] < 4 for c in need):
            ready += [(index,) + job for job in due()]
            now += 0.5
        ready += [(index, 4, c) for c in need]
        now = max([now] + [arrived[c, 3] for c in need]) + GRADS
        for k in range(ticks):
            beside += [(index * ticks + k,) + job for job in due()]
            now += TICK
    return head, ready, beside


def main_kernel(
    shards, cols,
    key_ref, left_ref, right_ref, mean_l_ref, var_l_ref, mean_r_ref, var_r_ref, in_ref, gr_ref,
    raw_ref,
    table, wide, weights, means, variances, keep, away, pair, land, low, step, acc, pieces,
    load, held, xs, xr, zs, zr, gs, gr, ys, yr, ps, pr, base_ref,
):
    me = lax.axis_index("proj")
    rest = shards // 2
    x, z = lax.rem(me, 2), me // 2
    n, tok, w = in_ref.shape
    chunks = n // PAIR
    total = 2 * chunks
    groups = n // GROUP
    piece = tok // rest
    partner = z * 2 + (1 - x)
    others = [lax.rem(z + d, rest) for d in range(1, rest)]
    down_row = w + 2 * RANK

    def span(start, size):
        return pl.ds(pl.multiple_of(start, 16), size)

    def loaded(source, c, slot):
        return pltpu.make_async_copy(
            source.at[pl.ds(c * PAIR, PAIR)], wide.at[slot], load.at[slot]
        )

    for c in range(SLOTS):
        loaded(in_ref, c, c).start()

    seed4 = key_ref[0] * 4
    anchors = [scramble(seed4 + t) for t in range(4)]
    bands = w // RANK
    for i in range(bands):
        inner = (me * w + i * RANK) * cols
        base_ref[i] = anchors[1] + inner
        base_ref[bands + 2 + i] = anchors[2] + inner
    base_ref[bands] = anchors[0]
    base_ref[bands + 1] = anchors[3]

    part = w // 2
    moments = [
        pltpu.make_async_copy(mean_r_ref, means.at[0], held.at[0]),
        pltpu.make_async_copy(var_r_ref, variances.at[0], held.at[1]),
    ] + [
        pltpu.make_async_copy(
            (mean_l_ref, var_l_ref)[i // 2].at[pl.ds((i % 2) * part, part)],
            keep.at[total - 4 + i, pl.ds(0, part)], held.at[2 + i],
        )
        for i in range(4)
    ]
    for copy in moments:
        copy.start()

    barrier = pltpu.get_barrier_semaphore()
    for d in range(1, shards):
        pl.semaphore_signal(
            barrier, inc=1, device_id={"proj": lax.rem(me + d, shards)}, device_id_type=MESH
        )

    weights[0] = left_ref[...]
    weights[1] = right_ref[...].astype(jnp.float32).T.astype(jnp.bfloat16)
    pl.semaphore_wait(barrier, shards - 1)

    def remote(src, dst, send, recv, target):
        return pltpu.make_async_remote_copy(
            src_ref=src, dst_ref=dst, send_sem=send, recv_sem=recv,
            device_id={"proj": target}, device_id_type=MESH,
        )

    def first(c):
        return remote(away.at[c], pair.at[c], xs.at[c], xr.at[c], partner)

    def second(c, d):
        s = c * (rest - 1) + d - 1
        return remote(
            away.at[c, span(others[d - 1] * piece, piece)], land.at[s],
            zs.at[s], zr.at[s], others[d - 1] * 2 + x,
        )

    def third(c, d):
        s = c * (rest - 1) + d - 1
        where = span((c % chunks) * PAIR * tok + x * tok + z * piece, piece)
        return remote(
            low.at[c // chunks, where], low.at[c // chunks, where],
            gs.at[s], gr.at[s], others[d - 1] * 2 + x,
        )

    def fourth(c):
        where = span((c % chunks) * PAIR * tok + x * tok, tok)
        return remote(
            low.at[c // chunks, where], low.at[c // chunks, where], ys.at[c], yr.at[c], partner
        )

    def job0(c):
        first(c).start()

    def job1(c):
        first(c).wait_recv()
        first(c).wait_send()
        away[c] = (keep[c] + pair[c].astype(jnp.float32)).astype(jnp.bfloat16)
        for d in range(1, rest):
            second(c, d).start()

    def job2(c):
        for d in range(1, rest):
            second(c, d).wait_recv()
        summed = away[c, span(z * piece, piece), :].astype(jnp.float32)
        for d in range(1, rest):
            summed = summed + land[c * (rest - 1) + d - 1].astype(jnp.float32)
        where = span((c % chunks) * PAIR * tok + x * tok + z * piece, piece)
        low[c // chunks, where, :] = (UPDATE_MULTIPLIER * summed).astype(jnp.bfloat16)
        for d in range(1, rest):
            third(c, d).start()

    def job3(c):
        for d in range(1, rest):
            third(c, d).wait_recv()
        fourth(c).start()

    def job4(c):
        fourth(c).wait_recv()

    def run(jobs, tick):
        for when in sorted(set(job[0] for job in jobs)):
            @pl.when(tick == when)
            def _():
                for _, stage, c in [job for job in jobs if job[0] == when]:
                    (job0, job1, job2, job3, job4)[stage](c)

    local = lax.broadcasted_iota(jnp.int32, (STEP, WIDE), 0) * cols + lax.broadcasted_iota(
        jnp.int32, (STEP, WIDE), 1
    )
    run_cols = 4 * WIDE
    per_row = cols // run_cols
    units = ((w + RANK) // STEP) * per_row
    per_chunk = -(-units // total)

    def make_unit(u):
        band = u // per_row
        left = lax.rem(u, per_row) * run_cols
        base = base_ref[band // (RANK // STEP)] + lax.rem(band, RANK // STEP) * (STEP * cols) + left
        for j in range(4):
            table[
                span(band * STEP, STEP), pl.ds(pl.multiple_of(left + j * WIDE, WIDE), WIDE)
            ] = signs(local + (base + j * WIDE))

    ticks = cols // TILE
    head_jobs, ready_jobs, pass_jobs = plan(total, 2 * groups, ticks)

    def head(c, carry):
        run(head_jobs, c)

        @pl.when(c == total // 2)
        def _():
            for copy in moments:
                copy.wait()
            for i in range(4):
                (means, variances)[i // 2][1, :, (i % 2) * part : (i % 2 + 1) * part] = keep[
                    total - 4 + i, 0:part, :
                ].T

        slot = lax.rem(c, SLOTS)
        loaded(in_ref, 0, slot).wait()
        which = c // chunks

        away[c] = jnp.dot(
            wide[slot, 1 - x], weights[which], preferred_element_type=jnp.float32
        ).astype(jnp.bfloat16)
        keep[c] = jnp.dot(wide[slot, x], weights[which], preferred_element_type=jnp.float32)
        for j in range(per_chunk):
            make_unit(lax.rem(c * per_chunk + j, units))
        ahead = c + SLOTS

        @pl.when(ahead < chunks)
        def _():
            loaded(in_ref, ahead, slot).start()

        @pl.when((ahead >= chunks) & (ahead < total))
        def _():
            loaded(gr_ref, ahead - chunks, slot).start()

        @pl.when(ahead >= total)
        def _():
            loaded(gr_ref, ahead - total, slot).start()

        return carry

    lax.fori_loop(0, total, head, 0)

    def grads(phase, group):
        mean, var = means.at[phase], variances.at[phase]

        def sample(i, carry):
            grad = lax.dot_general(
                low[phase, span((group * GROUP + i) * tok, tok), :],
                wide[i // PAIR, lax.rem(i, PAIR)],
                (((0,), (0,)), ((), ())), preferred_element_type=jnp.float32,
            )
            step[span(i * RANK, RANK), :] = (
                (0.9 * mean[...] + 0.1 * grad)
                * lax.rsqrt(0.999 * var[...] + 0.001 * grad * grad)
            ).astype(jnp.bfloat16)
            return carry

        lax.fori_loop(0, GROUP, sample, 0)

    def shared(group, d):
        target = lax.rem(me + d, shards)
        s = group * (shards - 1) + d - 1
        return remote(acc.at[group, target], pieces.at[group, d - 1], ps.at[s], pr.at[s], target)

    fresh_row = w + RANK
    fresh = (w + RANK) // groups
    width = w
    near = lax.broadcasted_iota(jnp.int32, (STEP, TILE), 0) * cols + lax.broadcasted_iota(
        jnp.int32, (STEP, TILE), 1
    )

    def project(phase, group):
        row0 = phase * down_row
        side0 = w + phase * RANK

        def tile(k, carry):
            run(pass_jobs, (phase * groups + group) * ticks + k)
            k = lax.rem((me * w) // TILE + 1 + k, ticks)
            col = pl.ds(pl.multiple_of(k * TILE, TILE), TILE)
            mixed = jnp.dot(
                step[...], table[row0 : row0 + w, col], preferred_element_type=jnp.float32
            )
            side = table[side0 : side0 + RANK, col].astype(jnp.float32)
            for i in range(GROUP):
                line = jnp.sum(mixed[i * RANK : (i + 1) * RANK] * side, axis=0, keepdims=True)
                for s in range(TILE // width):
                    shard, lanes = k * (TILE // width) + s, pl.ds(0, width)
                    part = line[:, s * width : (s + 1) * width]
                    if phase == 0:
                        acc[group, shard, i : i + 1, lanes] = part
                    else:
                        acc[group, shard, i : i + 1, lanes] = (
                            acc[group, shard, i : i + 1, lanes] + part
                        )
            if phase == 0:
                for r in range(0, fresh, STEP):
                    row = fresh_row + group * fresh + r
                    base = base_ref[row // RANK] + (lax.rem(row, RANK) * cols + k * TILE)
                    table[span(row, STEP), col] = signs(near + base)
            else:
                for s in range(TILE // width):
                    d = lax.rem(k * (TILE // width) + s - me + shards, shards)

                    @pl.when(d > 0)
                    def _():
                        shared(group, d).start()
            return carry

        lax.fori_loop(0, ticks, tile, 0)

    for phase in range(2):
        source = (gr_ref, in_ref)[phase]

        def one_pass(group, carry):
            run(ready_jobs, phase * groups + group)
            for slot in range(SLOTS):
                loaded(source, 0, slot).wait()
            grads(phase, group)

            @pl.when(group + 1 < groups)
            def _():
                for slot in range(SLOTS):
                    loaded(source, (group + 1) * SLOTS + slot, slot).start()

            if phase == 0:
                @pl.when(group + 1 == groups)
                def _():
                    for slot in range(SLOTS):
                        loaded(in_ref, slot, slot).start()

            project(phase, group)
            return carry

        lax.fori_loop(0, groups, one_pass, 0)

    for group in range(groups):
        for d in range(1, shards):
            shared(group, d).wait_recv()
        raw = acc[group, me]
        for d in range(1, shards):
            raw = raw + pieces[group, d - 1]
        raw_ref[group] = raw
    for c in range(total):
        fourth(c).wait_send()
        for d in range(1, rest):
            second(c, d).wait_send()
            third(c, d).wait_send()
    for group in range(groups):
        for d in range(1, shards):
            shared(group, d).wait_send()


def main(key, left, right, mean_l, var_l, mean_r, var_r, wide_in, wide_gr, shards, cols):
    n, tok, w = wide_in.shape
    rest = shards // 2
    groups = n // GROUP
    total = 2 * n // PAIR
    vmem = pl.BlockSpec(memory_space=pltpu.VMEM)
    hbm = pl.BlockSpec(memory_space=pl.ANY)
    dma = pltpu.SemaphoreType.DMA
    few, many = dma((total,)), dma((total * (rest - 1),))
    return pl.pallas_call(
        functools.partial(main_kernel, shards, cols),
        in_specs=[pl.BlockSpec(memory_space=pltpu.SMEM)] + [vmem] * 2 + [hbm] * 6,
        out_specs=vmem,
        out_shape=jax.ShapeDtypeStruct((groups, GROUP, w), jnp.float32),
        scratch_shapes=[
            pltpu.VMEM((2 * w + 2 * RANK, cols), jnp.bfloat16),
            pltpu.VMEM((SLOTS, PAIR, tok, w), jnp.bfloat16),
            pltpu.VMEM((2, w, RANK), jnp.bfloat16),
            pltpu.VMEM((2, RANK, w), jnp.float32),
            pltpu.VMEM((2, RANK, w), jnp.float32),
            pltpu.VMEM((total, tok, RANK), jnp.float32),
            pltpu.VMEM((total, tok, RANK), jnp.bfloat16),
            pltpu.VMEM((total, tok, RANK), jnp.bfloat16),
            pltpu.VMEM((total * (rest - 1), tok // rest, RANK), jnp.bfloat16),
            pltpu.VMEM((2, n * tok, RANK), jnp.bfloat16),
            pltpu.VMEM((GROUP * RANK, w), jnp.bfloat16),
            pltpu.VMEM((groups, shards, GROUP, w), jnp.float32),
            pltpu.VMEM((groups, shards - 1, GROUP, w), jnp.float32),
            dma((SLOTS,)), dma((6,)), few, few, many, many, many, many, few, few,
            dma((groups * (shards - 1),)), dma((groups * (shards - 1),)),
            pltpu.SMEM((2 * w // RANK + 2,), jnp.int32),
        ],
        compiler_params=pltpu.CompilerParams(
            collective_id=1, has_side_effects=True, vmem_limit_bytes=63 * 1024 * 1024
        ),
        cost_estimate=pl.CostEstimate(
            flops=4 * n * RANK * w * cols, bytes_accessed=8 * n * tok * w, transcendentals=0
        ),
        name="main",
    )(key, left, right, mean_l, var_l, mean_r, var_r, wide_in, wide_gr)


def finish_kernel(
    shards, langs, nval,
    raw_ref, lang_ref, tally_ref, val_ref,
    feat_ref, score_ref,
    message, notes, send, recv,
):
    me = lax.axis_index("proj")
    n, w = feat_ref.shape
    cols = shards * w
    barrier = pltpu.get_barrier_semaphore()
    for d in range(1, shards):
        pl.semaphore_signal(
            barrier, inc=1, device_id={"proj": lax.rem(me + d, shards)}, device_id_type=MESH
        )

    raw = jnp.concatenate([raw_ref[g] for g in range(raw_ref.shape[0])], axis=0)
    raw_low = raw.astype(jnp.bfloat16)
    ones = jnp.ones((16, w), jnp.bfloat16)
    both = (((1,), (1,)), ((), ()))
    own = jnp.zeros((n, nval), jnp.float32)
    square = jnp.zeros((n, nval), jnp.float32)
    count = jnp.zeros((n, 1), jnp.int32)
    for l in range(langs):
        val = val_ref[l]
        named = lang_ref[...] == l
        count = jnp.where(named, tally_ref[l], count)
        hot = jnp.where(named, jnp.float32(1.0), jnp.float32(0.0))
        own = own + hot * lax.dot_general(raw_low, val, both, preferred_element_type=jnp.float32)
        wide = val.astype(jnp.float32)
        sums = lax.dot_general(
            ones, (wide * wide).astype(jnp.bfloat16), both, preferred_element_type=jnp.float32
        )
        square = square + hot * sums[0:1]
    message[...] = jnp.zeros(message.shape, jnp.bfloat16)
    message[16 : 16 + n, :nval] = square.astype(jnp.bfloat16)
    message[:n, :nval] = own.astype(jnp.bfloat16)
    message[:n, nval:] = jnp.broadcast_to(
        jnp.sum(raw * raw, axis=1, keepdims=True), (n, message.shape[1] - nval)
    ).astype(jnp.bfloat16)
    pl.semaphore_wait(barrier, shards - 1)
    copies = []
    for d in range(1, shards):
        target = lax.rem(me + d, shards)
        copy = pltpu.make_async_remote_copy(
            src_ref=message, dst_ref=notes.at[d - 1],
            send_sem=send.at[d - 1], recv_sem=recv.at[d - 1],
            device_id={"proj": target}, device_id_type=MESH,
        )
        copy.start()
        copies.append(copy)
    total = message[...].astype(jnp.float32)
    for copy in copies:
        copy.wait_recv()
    for d in range(1, shards):
        total = total + notes[d - 1].astype(jnp.float32)
    inverse = lax.rsqrt(total[:n, nval : nval + 1] / cols + 1e-06)
    feat_ref[...] = raw * inverse
    rms = jnp.sqrt(total[16 : 16 + n, :nval] / cols + 1e-06)
    similar = total[:n, :nval] * inverse / (math.sqrt(cols) * rms)
    live = lax.broadcasted_iota(jnp.int32, (n, nval), 1) < count
    best = jnp.max(jnp.where(live, similar, jnp.float32(-1e30)), axis=1, keepdims=True)
    score_ref[...] = jnp.broadcast_to(best, score_ref.shape)
    for copy in copies:
        copy.wait_send()


def finish(raw, lang_of, tally, all_val, shards):
    groups, size, w = raw.shape
    n = groups * size
    langs, nval = all_val.shape[0], all_val.shape[1]
    vmem = pl.BlockSpec(memory_space=pltpu.VMEM)
    return pl.pallas_call(
        functools.partial(finish_kernel, shards, langs, nval),
        in_specs=[
            vmem, vmem, pl.BlockSpec(memory_space=pltpu.SMEM), vmem,
        ],
        out_specs=[vmem] * 2,
        out_shape=[
            jax.ShapeDtypeStruct((n, w), jnp.float32),
            jax.ShapeDtypeStruct((n, 128), jnp.float32),
        ],
        scratch_shapes=[
            pltpu.VMEM((32, nval + 128), jnp.bfloat16),
            pltpu.VMEM((shards - 1, 32, nval + 128), jnp.bfloat16),
            pltpu.SemaphoreType.DMA((shards - 1,)),
            pltpu.SemaphoreType.DMA((shards - 1,)),
        ],
        compiler_params=pltpu.CompilerParams(
            collective_id=0, has_side_effects=True, vmem_limit_bytes=32 * 1024 * 1024
        ),
        name="finish",
    )(raw, lang_of, tally, all_val)


def per_device(
    mapped_layer_arguments,
    loss_slope_at_result,
    left_lowrank_weights,
    right_lowrank_weights,
    mean_estimate_left,
    variance_estimate_left,
    mean_estimate_right,
    variance_estimate_right,
    heldout_sketched_slopes,
    tongue_label_per_example,
    heldout_example_tally,
    sketch_random_key,
):
    shards = lax.axis_size("proj")
    n, tok, w = mapped_layer_arguments.shape
    K = w * shards

    raw = main(
        sketch_random_key, left_lowrank_weights, right_lowrank_weights, mean_estimate_left,
        variance_estimate_left, mean_estimate_right, variance_estimate_right,
        mapped_layer_arguments, loss_slope_at_result, shards, K,
    )

    all_val = lax.all_gather(heldout_sketched_slopes, "lang", axis=0, tiled=True)
    features, scores = finish(
        raw, tongue_label_per_example, heldout_example_tally, all_val, shards
    )
    scores = scores[:, 0]
    return (features, scores)


def solution(mesh):
    in_specs = (
        P("lang", None, "proj"),
        P("lang", None, "proj"),
        P("proj", None),
        P(None, "proj"),
        P("proj", None),
        P("proj", None),
        P(None, "proj"),
        P(None, "proj"),
        P("lang", None, "proj"),
        P("lang", None),
        P(),
        P(),
    )
    out_specs = (P("lang", "proj"), P("lang"))
    return jax.shard_map(
        per_device, mesh=mesh, in_specs=in_specs, out_specs=out_specs, check_vma=False
    )
```
